128 devices in a mesh: req: 32 (over y, x, core), mlp: 4 (over z).
Axes of the slice: x: 4, y: 4, z: 4, core: 2. Of those that a mesh axis runs over, the one named last changes fastest.
Arguments:
- states: bfloat16 [8192, 2560], P('req')
- attn_gain: float32 [2560], replicated, may hold values from 0.1 to 1.9
- query_matrix: bfloat16 [2560, 2048], P(None, 'mlp')
- key_matrix: bfloat16 [2560, 1024], P(None, 'mlp')
- value_matrix: bfloat16 [2560, 1024], P(None, 'mlp'), may hold values from -0.125 to 0.125
- query_gain: float32 [256], replicated
- key_gain: float32 [256], replicated
- out_weight: bfloat16 [2048, 2560], P('mlp'), may hold values from -0.125 to 0.125
- post_gain: float32 [2560], replicated, may hold values from 0.1 to 1.9
- ffw_gain: float32 [2560], replicated, may hold values from 0.1 to 1.9
- gate_weight: bfloat16 [2560, 10240], P(None, 'req'), may hold values from -0.125 to 0.125
- up_weight: bfloat16 [2560, 10240], P(None, 'req'), may hold values from -0.125 to 0.125
- down_weight: bfloat16 [10240, 2560], P('req'), may hold values from -0.0625 to 0.0625
- post_ffw_gain: float32 [2560], replicated, may hold values from 0.1 to 1.9
- prefix_key_cache: bfloat16 [32, 512, 1024], P('req', None, 'mlp')
- prefix_value_cache: bfloat16 [32, 512, 1024], P('req', None, 'mlp'), may hold values from -6 to 6
- segment: int32 [8192], P('req'), may hold values from 0 to 15, as said below
- prefix_id: int32 [8192], P('req'), may hold values from 0 to 31, as said below
- owner_map: int32 [32], replicated, may hold values from 0 to 31, each once
Outputs:
- layer_out: bfloat16 [8192, 2560], P(('req', 'mlp'))
The draws below stay inside these ranges and needn't reach their ends.
Inputs may be any that keep to these rules, and one draw needn't show every extreme that they name: Within each block of 256 rows, equal segment values mark one request and occupy contiguous rows; requests hold 16 or 32 tokens. `prefix_id`: all tokens of one request name the same prefix group. In each block of 256 rows at most 32 rows name prefix groups of the same owner, and one prefix group is named by exactly 32 rows of every block.
All inputs are finite; a program needn't handle non-finite values.
Results may differ from the reference program's by a relative error of at most 0.017.
The reference program's roundings to bfloat16 on the way count: a program that leaves them out, or rounds other values in their place, can miss the bound.
Values may be sent and summed in bfloat16 or wider, within the bound.
A program may use at most 128 MiB of HBM per device.

```python
import math
import jax
import jax.numpy as jnp
from jax import lax

MODEL_WIDTH = 2560
FF = 10240
QUERY_HEADS = 8
KEY_VALUE_HEADS = 4
HEAD_SIZE = 256
TOKENS_PER_REQ = 256
PREFIX_LENGTH = 512
CAP = 32
SUFFIX_TOKENS = 8192
PREFIX_NUMBER = 32


def draw_states(key, part):
    sampled_items = jnp.clip(jax.random.normal(jax.random.fold_in(key, 101), (SUFFIX_TOKENS, MODEL_WIDTH), jnp.float32), -6.0, 6.0)
    return sampled_items.astype(jnp.bfloat16)


def draw_query_matrix(key, part):
    sampled_items = jax.random.normal(jax.random.fold_in(key, 201), (MODEL_WIDTH, QUERY_HEADS * HEAD_SIZE), jnp.float32)
    return (sampled_items / math.sqrt(MODEL_WIDTH)).astype(jnp.bfloat16)


def draw_key_matrix(key, part):
    sampled_items = jax.random.normal(jax.random.fold_in(key, 301), (MODEL_WIDTH, KEY_VALUE_HEADS * HEAD_SIZE), jnp.float32)
    return (sampled_items / math.sqrt(MODEL_WIDTH)).astype(jnp.bfloat16)


def draw_query_gain(key, part):
    return jax.random.uniform(jax.random.fold_in(key, 401), (HEAD_SIZE,), jnp.float32, 0.6, 1.6)


def draw_key_gain(key, part):
    return jax.random.uniform(jax.random.fold_in(key, 501), (HEAD_SIZE,), jnp.float32, 0.6, 1.6)


def draw_prefix_key_cache(key, part):
    sampled_items = jnp.clip(jax.random.normal(jax.random.fold_in(key, 601), (PREFIX_NUMBER, PREFIX_LENGTH, KEY_VALUE_HEADS * HEAD_SIZE), jnp.float32), -6.0, 6.0)
    return sampled_items.astype(jnp.bfloat16)


def request_layout(key):
    base = jax.random.fold_in(key, 777)
    device_count = SUFFIX_TOKENS // TOKENS_PER_REQ
    block_count = TOKENS_PER_REQ // CAP
    hot_group = jax.random.randint(jax.random.fold_in(base, 1), (), 0, PREFIX_NUMBER)
    device_keys = jax.random.split(jax.random.fold_in(base, 2), device_count)
    others = jax.vmap(lambda one_key: jax.random.permutation(one_key, PREFIX_NUMBER - 1))(device_keys)[:, :block_count - 1]
    others = others + (others >= hot_group).astype(others.dtype)
    hot_at = jax.random.randint(jax.random.fold_in(base, 3), (device_count,), 0, block_count)
    block_index = jnp.arange(block_count, dtype=jnp.int32)
    pick = jnp.clip(block_index[None, :] - (block_index[None, :] > hot_at[:, None]).astype(jnp.int32), 0, block_count - 2)
    chosen = jnp.take_along_axis(others, pick, axis=1)
    block_group = jnp.where(block_index[None, :] == hot_at[:, None], hot_group, chosen)
    split_flag = jax.random.randint(jax.random.fold_in(base, 4), (device_count, block_count), 0, 2)
    offset = jnp.arange(CAP, dtype=jnp.int32)
    seg_ids = 2 * block_index[None, :, None] + split_flag[:, :, None] * (offset[None, None, :] >= CAP // 2).astype(jnp.int32)
    group_ids = jnp.broadcast_to(block_group[:, :, None], (device_count, block_count, CAP))
    return (seg_ids.reshape(SUFFIX_TOKENS).astype(jnp.int32), group_ids.reshape(SUFFIX_TOKENS).astype(jnp.int32))


def draw_segment(key, part):
    return request_layout(key)[0]


def draw_prefix_id(key, part):
    return request_layout(key)[1]


def levels(rng, shape, cuts, smallest, high):
    gain, own = 1.0, jax.random.fold_in(rng, 6)
    for axis_at, blocks in cuts:
        draws = jnp.exp(jax.random.uniform(jax.random.fold_in(own, axis_at), (blocks,), jnp.float32, smallest / len(cuts), high / len(cuts)))
        gain = gain * jnp.repeat(draws, shape[axis_at] // blocks).reshape([-1 if axis == axis_at else 1 for axis in range(len(shape))])
    return gain


def normal_values(key, extent, deviation, reach, shards=(), held_as=jnp.bfloat16):
    factor_of = levels(key, extent, shards, -0.22, 0.18) if shards else 1.0
    drawn = jax.random.normal(key, extent, jnp.float32) * deviation * factor_of
    return jnp.minimum(jnp.maximum(drawn, -reach), reach).astype(held_as)


def setup_inputs(seed: int = 0) -> dict:
    keys = jax.random.split(jax.random.key(seed), 20)
    return {
        "states": draw_states(jax.random.fold_in(keys[19], 71), 0),
        "attn_gain": jnp.clip(1.0 + 0.18 * jax.random.normal(keys[1], (MODEL_WIDTH,), jnp.float32), 0.1, 1.9),
        "query_matrix": draw_query_matrix(jax.random.fold_in(keys[19], 71), 0),
        "key_matrix": draw_key_matrix(jax.random.fold_in(keys[19], 71), 0),
        "value_matrix": normal_values(keys[4], (MODEL_WIDTH, KEY_VALUE_HEADS * HEAD_SIZE), MODEL_WIDTH ** -0.5, 0.125, ((1, 4),)),
        "query_gain": draw_query_gain(jax.random.fold_in(keys[19], 71), 0),
        "key_gain": draw_key_gain(jax.random.fold_in(keys[19], 71), 0),
        "out_weight": normal_values(keys[7], (QUERY_HEADS * HEAD_SIZE, MODEL_WIDTH), (QUERY_HEADS * HEAD_SIZE) ** -0.5, 0.125, ((0, 4),)),
        "post_gain": jnp.clip(1.0 + 0.18 * jax.random.normal(keys[8], (MODEL_WIDTH,), jnp.float32), 0.1, 1.9),
        "ffw_gain": jnp.clip(1.0 + 0.18 * jax.random.normal(keys[9], (MODEL_WIDTH,), jnp.float32), 0.1, 1.9),
        "gate_weight": normal_values(keys[10], (MODEL_WIDTH, FF), MODEL_WIDTH ** -0.5, 0.125, ((1, 32),)),
        "up_weight": normal_values(keys[11], (MODEL_WIDTH, FF), MODEL_WIDTH ** -0.5, 0.125, ((1, 32),)),
        "down_weight": normal_values(keys[12], (FF, MODEL_WIDTH), FF ** -0.5, 0.0625, ((0, 32),)),
        "post_ffw_gain": jnp.clip(1.0 + 0.18 * jax.random.normal(keys[13], (MODEL_WIDTH,), jnp.float32), 0.1, 1.9),
        "prefix_key_cache": draw_prefix_key_cache(jax.random.fold_in(keys[19], 71), 0),
        "prefix_value_cache": normal_values(keys[15], (PREFIX_NUMBER, PREFIX_LENGTH, KEY_VALUE_HEADS * HEAD_SIZE), 1.0, 6.0, ((0, 32), (2, 4))),
        "segment": draw_segment(jax.random.fold_in(keys[19], 71), 0),
        "prefix_id": draw_prefix_id(jax.random.fold_in(keys[19], 71), 0),
        "owner_map": jax.random.permutation(keys[18], PREFIX_NUMBER).astype(jnp.int32),
    }


EPS = 1e-06

def normed(values_in, gain_vec):
    return values_in * lax.rsqrt(lax.optimization_barrier(jnp.mean(values_in * values_in, axis=-1, keepdims=True)) + EPS) * gain_vec

def widened(array_in):
    return lax.optimization_barrier(array_in.astype(jnp.bfloat16)).astype(jnp.float32)

def local_attention(query_rows, key_rows, value_rows, segment_rows, score_scale):
    scores = jnp.einsum('tgqd,sgd->gqts', query_rows.astype(jnp.float32), key_rows.astype(jnp.float32)) * score_scale
    row_count = segment_rows.shape[0]
    token_position = jnp.arange(row_count, dtype=jnp.int32)
    allowed = (segment_rows[:, None] == segment_rows[None, :]) & (token_position[:, None] >= token_position[None, :])
    scores = jnp.where(allowed, scores, -jnp.inf)
    row_max = lax.optimization_barrier(jnp.max(scores, axis=-1, keepdims=True))
    powers = jnp.exp(scores - row_max)
    row_sum = lax.optimization_barrier(jnp.sum(powers, axis=-1, keepdims=True))
    weights = widened(powers / row_sum)
    mixed = jnp.einsum('gqts,sgd->tgqd', weights, value_rows.astype(jnp.float32))
    log_total = jnp.transpose((row_max + jnp.log(row_sum))[..., 0], (2, 0, 1))
    return (mixed, log_total)

def reference(states, attn_gain, query_matrix, key_matrix, value_matrix, query_gain, key_gain, out_weight, post_gain, ffw_gain, gate_weight, up_weight, down_weight, post_ffw_gain, prefix_key_cache, prefix_value_cache, segment, prefix_id, owner_map):
    query_group_width = QUERY_HEADS // KEY_VALUE_HEADS
    score_scale = 1.0 / math.sqrt(HEAD_SIZE)
    block_list = SUFFIX_TOKENS // TOKENS_PER_REQ
    states_f = states.astype(jnp.float32)
    normalized_input = normed(states_f, attn_gain).astype(jnp.bfloat16)
    unnormed_queries = jnp.dot(normalized_input, query_matrix, preferred_element_type=jnp.float32).reshape(SUFFIX_TOKENS, KEY_VALUE_HEADS, query_group_width, HEAD_SIZE)
    query_vectors = normed(unnormed_queries, query_gain).astype(jnp.bfloat16)
    unnormed_keys = jnp.dot(normalized_input, key_matrix, preferred_element_type=jnp.float32).reshape(SUFFIX_TOKENS, KEY_VALUE_HEADS, HEAD_SIZE)
    key_vectors = normed(unnormed_keys, key_gain).astype(jnp.bfloat16)
    value_vectors = jnp.dot(normalized_input, value_matrix, preferred_element_type=jnp.float32).astype(jnp.bfloat16).reshape(SUFFIX_TOKENS, KEY_VALUE_HEADS, HEAD_SIZE)

    def single_block(pieces):
        return local_attention(pieces[0], pieces[1], pieces[2], pieces[3], score_scale)
    suffix_output, suffix_log_sum = lax.map(single_block, (query_vectors.reshape(block_list, TOKENS_PER_REQ, KEY_VALUE_HEADS, query_group_width, HEAD_SIZE), key_vectors.reshape(block_list, TOKENS_PER_REQ, KEY_VALUE_HEADS, HEAD_SIZE), value_vectors.reshape(block_list, TOKENS_PER_REQ, KEY_VALUE_HEADS, HEAD_SIZE), segment.reshape(block_list, TOKENS_PER_REQ)))
    suffix_output = suffix_output.reshape(SUFFIX_TOKENS, KEY_VALUE_HEADS, query_group_width, HEAD_SIZE)
    suffix_log_sum = suffix_log_sum.reshape(SUFFIX_TOKENS, KEY_VALUE_HEADS, query_group_width)
    cache_row = owner_map[prefix_id].astype(jnp.int32)
    query_f = query_vectors.astype(jnp.float32)

    def visit(carry, selected_index):
        stored_keys = prefix_key_cache[selected_index].astype(jnp.float32).reshape(PREFIX_LENGTH, KEY_VALUE_HEADS, HEAD_SIZE)
        stored_values = prefix_value_cache[selected_index].astype(jnp.float32).reshape(PREFIX_LENGTH, KEY_VALUE_HEADS, HEAD_SIZE)
        scores = jnp.einsum('tgqd,kgd->tgqk', query_f, stored_keys) * score_scale
        row_max = lax.optimization_barrier(jnp.max(scores, axis=-1, keepdims=True))
        powers = jnp.exp(scores - row_max)
        row_sum = lax.optimization_barrier(jnp.sum(powers, axis=-1, keepdims=True))
        weights = widened(powers / row_sum)
        mixed = widened(jnp.einsum('tgqk,kgd->tgqd', weights, stored_values))
        log_total = row_max[..., 0] + jnp.log(row_sum[..., 0])
        chosen = cache_row == selected_index
        new_out = jnp.where(chosen[:, None, None, None], mixed, carry[0])
        new_lse = jnp.where(chosen[:, None, None], log_total, carry[1])
        return ((new_out, new_lse), None)
    initial_state = (jnp.zeros((SUFFIX_TOKENS, KEY_VALUE_HEADS, query_group_width, HEAD_SIZE), jnp.float32), jnp.zeros((SUFFIX_TOKENS, KEY_VALUE_HEADS, query_group_width), jnp.float32))
    (prefix_out, prefix_lse), _ = lax.scan(visit, initial_state, jnp.arange(PREFIX_NUMBER, dtype=jnp.int32))
    blend = jax.nn.sigmoid(prefix_lse - suffix_log_sum)[..., None]
    attended = (blend * prefix_out + (1.0 - blend) * suffix_output).astype(jnp.bfloat16).reshape(SUFFIX_TOKENS, QUERY_HEADS * HEAD_SIZE)
    attn_sum = jnp.dot(attended, out_weight, preferred_element_type=jnp.float32)
    residual = states_f + normed(attn_sum, post_gain)
    ffw_in = normed(residual, ffw_gain).astype(jnp.bfloat16)
    gate_proj = jnp.dot(ffw_in, gate_weight, preferred_element_type=jnp.float32)
    up_proj = jnp.dot(ffw_in, up_weight, preferred_element_type=jnp.float32)
    hidden = (jax.nn.gelu(gate_proj, approximate=True) * up_proj).astype(jnp.bfloat16)
    down_sum = jnp.dot(hidden, down_weight, preferred_element_type=jnp.float32)
    return (residual + normed(down_sum, post_ffw_gain)).astype(jnp.bfloat16)
```

```python
import jax
import jax.numpy as jnp
from jax import lax
from jax.sharding import PartitionSpec as P

CAP = 32


EPS = 1e-06


def normed(values_in, gain_vec):
    return (
        values_in
        * lax.rsqrt(jnp.mean(values_in * values_in, axis=-1, keepdims=True) + EPS)
        * gain_vec
    )


def local_attention(query_rows, key_rows, value_rows, segment_rows, score_scale):
    scores = (
        jnp.einsum("tgqd,sgd->gqts", query_rows, key_rows, preferred_element_type=jnp.float32)
        * score_scale
    )
    row_count = segment_rows.shape[0]
    token_position = jnp.arange(row_count, dtype=jnp.int32)
    allowed = (segment_rows[:, None] == segment_rows[None, :]) & (
        token_position[:, None] >= token_position[None, :]
    )
    scores = jnp.where(allowed, scores, -jnp.inf)
    row_max = jnp.max(scores, axis=-1, keepdims=True)
    powers = jnp.exp(scores - row_max)
    row_sum = jnp.sum(powers, axis=-1, keepdims=True)
    weights = (powers / row_sum).astype(jnp.bfloat16)
    mixed = jnp.einsum("gqts,sgd->tgqd", weights, value_rows, preferred_element_type=jnp.float32)
    log_total = jnp.transpose((row_max + jnp.log(row_sum))[..., 0], (2, 0, 1))
    return (mixed, log_total)


def prefix_partials(incoming, stored_keys, stored_values, score_scale):
    sources, slot_count, head_cols = incoming.shape
    kv_heads = stored_keys.shape[1]
    head_dim = stored_keys.shape[2]
    query_group_width = head_cols // (kv_heads * head_dim)
    query_rows = incoming.reshape(sources * slot_count, kv_heads, query_group_width, head_dim)
    scores = (
        jnp.einsum("rgqd,kgd->rgqk", query_rows, stored_keys, preferred_element_type=jnp.float32)
        * score_scale
    )
    row_max = jnp.max(scores, axis=-1, keepdims=True)
    powers = jnp.exp(scores - row_max)
    row_sum = jnp.sum(powers, axis=-1, keepdims=True)
    weights = (powers / row_sum).astype(jnp.bfloat16)
    mixed = jnp.einsum("rgqk,kgd->rgqd", weights, stored_values, preferred_element_type=jnp.float32)
    mixed = lax.optimization_barrier(mixed.astype(jnp.bfloat16)).astype(jnp.float32)
    log_total = row_max[..., 0] + jnp.log(row_sum[..., 0])
    return (
        mixed.reshape(sources, slot_count, head_cols),
        log_total.reshape(sources, slot_count, kv_heads * query_group_width),
    )


def body(
    states,
    attn_gain,
    query_matrix,
    key_matrix,
    value_matrix,
    query_gain,
    key_gain,
    out_weight,
    post_gain,
    ffw_gain,
    gate_weight,
    up_weight,
    down_weight,
    post_ffw_gain,
    prefix_key_cache,
    prefix_value_cache,
    segment,
    prefix_id,
    owner_map,
):
    row_count = states.shape[0]
    head_dim = query_gain.shape[0]
    kv_heads = key_matrix.shape[1] // head_dim
    head_cols = query_matrix.shape[1]
    query_group_width = head_cols // (kv_heads * head_dim)
    score_scale = head_dim ** (-0.5)
    req_count = lax.axis_size("req")
    mlp_count = lax.axis_size("mlp")
    mlp_index = lax.axis_index("mlp")
    quarter = row_count // mlp_count
    states_f = states.astype(jnp.float32)
    normalized_input = normed(states_f, attn_gain).astype(jnp.bfloat16)
    unnormed_queries = jnp.dot(
        normalized_input, query_matrix, preferred_element_type=jnp.float32
    ).reshape(row_count, kv_heads, query_group_width, head_dim)
    query_vectors = normed(unnormed_queries, query_gain).astype(jnp.bfloat16)
    unnormed_keys = jnp.dot(
        normalized_input, key_matrix, preferred_element_type=jnp.float32
    ).reshape(row_count, kv_heads, head_dim)
    key_vectors = normed(unnormed_keys, key_gain).astype(jnp.bfloat16)
    value_vectors = (
        jnp.dot(normalized_input, value_matrix, preferred_element_type=jnp.float32)
        .astype(jnp.bfloat16)
        .reshape(row_count, kv_heads, head_dim)
    )
    prefix_count = owner_map.shape[0]
    prefix_onehot = (
        prefix_id[:, None] == jnp.arange(prefix_count, dtype=jnp.int32)[None, :]
    ).astype(jnp.int32)
    target = jnp.sum(prefix_onehot * owner_map[None, :], axis=1)
    to_owner = (target[:, None] == jnp.arange(req_count, dtype=jnp.int32)[None, :]).astype(
        jnp.float32
    )
    token_position = jnp.arange(row_count, dtype=jnp.int32)
    earlier = (token_position[:, None] > token_position[None, :]).astype(jnp.float32)
    counts = jnp.dot(earlier, to_owner, precision=lax.Precision.HIGHEST)
    slot_index = jnp.sum(to_owner * counts, axis=1).astype(jnp.int32)
    place_row = target * CAP + slot_index
    placing = (place_row[None, :] == jnp.arange(req_count * CAP, dtype=jnp.int32)[:, None]).astype(
        jnp.bfloat16
    )
    outgoing = (
        jnp.dot(
            placing, query_vectors.reshape(row_count, head_cols), preferred_element_type=jnp.float32
        )
        .astype(jnp.bfloat16)
        .reshape(req_count, CAP, head_cols)
    )
    stored_keys = prefix_key_cache[0].reshape(-1, kv_heads, head_dim)
    stored_values = prefix_value_cache[0].reshape(-1, kv_heads, head_dim)
    suffix_output, suffix_log_sum = local_attention(
        query_vectors, key_vectors, value_vectors, segment, score_scale
    )
    mixed, log_total = prefix_partials(
        lax.all_to_all(outgoing, "req", split_axis=0, concat_axis=0, tiled=True),
        stored_keys,
        stored_values,
        score_scale,
    )
    back_out = lax.all_to_all(
        mixed.astype(jnp.bfloat16), "req", split_axis=0, concat_axis=0, tiled=True
    ).astype(mixed.dtype)
    back_lse = lax.all_to_all(
        log_total.astype(jnp.bfloat16), "req", split_axis=0, concat_axis=0, tiled=True
    ).astype(log_total.dtype)
    prefix_out = back_out.reshape(req_count * CAP, head_cols)[place_row].reshape(
        row_count, kv_heads, query_group_width, head_dim
    )
    prefix_lse = back_lse.reshape(req_count * CAP, kv_heads * query_group_width)[place_row].reshape(
        row_count, kv_heads, query_group_width
    )
    prefix_out, prefix_lse = (prefix_out, prefix_lse)
    blend = jax.nn.sigmoid(prefix_lse - suffix_log_sum)[..., None]
    attended = (
        (blend * prefix_out + (1.0 - blend) * suffix_output)
        .astype(jnp.bfloat16)
        .reshape(row_count, head_cols)
    )
    partial_value = jnp.dot(attended, out_weight, preferred_element_type=jnp.float32)
    summed = lax.psum_scatter(
        partial_value.astype(jnp.bfloat16), "mlp", scatter_dimension=0, tiled=True
    ).astype(jnp.float32)
    own_rows = lax.dynamic_slice_in_dim(states_f, mlp_index * quarter, quarter, 0)
    residual = own_rows + normed(summed, post_gain)
    ffw_in = normed(residual, ffw_gain).astype(jnp.bfloat16)
    piece = lax.all_gather(ffw_in, "req", axis=0, tiled=True)
    gate_proj = jnp.dot(piece, gate_weight, preferred_element_type=jnp.float32)
    up_proj = jnp.dot(piece, up_weight, preferred_element_type=jnp.float32)
    hidden = (jax.nn.gelu(gate_proj, approximate=True) * up_proj).astype(jnp.bfloat16)
    down_sum = lax.psum_scatter(
        jnp.dot(hidden, down_weight, preferred_element_type=jnp.float32).astype(jnp.bfloat16),
        "req",
        scatter_dimension=0,
        tiled=True,
    ).astype(jnp.float32)
    return (residual + normed(down_sum, post_ffw_gain)).astype(jnp.bfloat16)


def solution(mesh):
    return jax.shard_map(
        body,
        mesh=mesh,
        in_specs=(
            P("req", None),
            P(),
            P(None, "mlp"),
            P(None, "mlp"),
            P(None, "mlp"),
            P(),
            P(),
            P("mlp", None),
            P(),
            P(),
            P(None, "req"),
            P(None, "req"),
            P("req", None),
            P(),
            P("req", None, "mlp"),
            P("req", None, "mlp"),
            P("req"),
            P("req"),
            P(),
        ),
        out_specs=P(("req", "mlp"), None),
        check_vma=False,
    )
```
